32 devices in a mesh: frame: 16 (over z, y, core), head: 2 (over x).
Axes of the slice: x: 2, y: 2, z: 4, core: 2. Of those that a mesh axis runs over, the one named last changes fastest.
Arguments:
- tokens: bfloat16 [16384, 3072], P('frame'), may hold values from -6 to 6
- qkv_weight: bfloat16 [3, 3072, 3072], P(None, None, 'head'), may hold values from -0.109375 to 0.109375
- query_gain: float32 [128], replicated, may hold values from 0.1 to 1.9
- key_gain: float32 [128], replicated, may hold values from 0.1 to 1.9
- labels: int32 [24], P('head'), may hold values from 0 to 1, as said below
- space_mask: int32 [24, 16, 48], P('head'), may hold values from 0 to 1, as said below
- time_mask: int32 [24, 2, 2], P('head'), may hold values from 0 to 1, as said below
Outputs:
- attended: bfloat16 [16384, 3072], P(('frame', 'head'))
The draws below stay inside these ranges and needn't reach their ends.
Inputs may be any that keep to these rules, and one draw needn't show every extreme that they name: `labels`: among heads 3 * j, 3 * j + 1 and 3 * j + 2 exactly one is temporal. space_mask[h, a, 16 + a] = 1 for every head and query block. For each head, at most 8 key blocks of the previous frame (b < 16) are allowed for some query block, and at most 8 of the next frame (b >= 32); some head reaches 8 on each side. time_mask[h, a, a] = 1 for every head and query block.
All inputs are finite; a program needn't handle non-finite values.
Results may differ from the reference program's by a relative error of at most 0.0073.
Values may be sent and summed in bfloat16 or wider, within the bound.
A program may use at most 192 MiB of HBM per device.

```python
import math
import jax
import jax.numpy as jnp
from jax import lax

D = 3072
HEADS = 24
HEAD_DIM = 128
TOK_FRAME = 1024
STRIP = 8
BLOCK = 64
FRAMES = 16
TOKENS = 16384
QBLOCKS = 16
TBLOCKS = 2
NEAR_MAX = 8


def draw_labels(key, part):
    groups = HEADS // 3
    chosen = jax.random.randint(key, (groups,), 0, 3)
    marks = jnp.arange(3, dtype=jnp.int32)[None, :] == chosen[:, None]
    return marks.astype(jnp.int32).reshape(HEADS)


def draw_space_mask(key, part):
    keys = jax.random.split(jax.random.fold_in(key, 11), 7)
    density = jax.random.randint(keys[0], (HEADS, 1, 1), 2, 9)
    middle = jax.random.randint(keys[1], (HEADS, QBLOCKS, QBLOCKS), 0, 10) < density
    diagonal = jnp.eye(QBLOCKS, dtype=jnp.int32)[None] == 1
    middle = middle | diagonal
    counts = jax.random.randint(keys[2], (2, HEADS), 1, NEAR_MAX + 1)
    fullest = jax.random.randint(keys[3], (2,), 0, HEADS)
    counts = jnp.where(jnp.arange(HEADS, dtype=jnp.int32)[None, :] == fullest[:, None], NEAR_MAX, counts)
    scores = jax.random.randint(keys[4], (2, HEADS, QBLOCKS), 0, 1 << 20) * QBLOCKS + jnp.arange(QBLOCKS, dtype=jnp.int32)
    ranking = jnp.argsort(jnp.argsort(scores, axis=-1), axis=-1)
    column_on = ranking < counts[:, :, None]
    random_live = jax.random.randint(keys[5], (2, HEADS, QBLOCKS, QBLOCKS), 0, 10) < density[None]
    forced_row = jax.random.randint(keys[6], (2, HEADS, QBLOCKS), 0, QBLOCKS)
    row_ids = jnp.arange(QBLOCKS, dtype=jnp.int32)[None, None, :, None]
    forced = row_ids == forced_row[:, :, None, :]
    near = column_on[:, :, None, :] & (random_live | forced)
    whole = jnp.concatenate([near[0], middle, near[1]], axis=2)
    return whole.astype(jnp.int32)


def draw_time_mask(key, part):
    keys = jax.random.split(jax.random.fold_in(key, 23), 2)
    density = jax.random.randint(keys[0], (HEADS, 1, 1), 2, 9)
    live = jax.random.randint(keys[1], (HEADS, TBLOCKS, TBLOCKS), 0, 10) < density
    live = live | (jnp.eye(TBLOCKS, dtype=jnp.int32)[None] == 1)
    return live.astype(jnp.int32)


def shard_levels(stream_key, shape, shards, least, high):
    loudness = 1.0
    for position, blocks in shards:
        heights = jax.random.uniform(jax.random.fold_in(jax.random.fold_in(stream_key, 6), position), (blocks,), jnp.float32, least / len(shards), high / len(shards))
        loudness = loudness * jnp.repeat(jnp.exp(heights), shape[position] // blocks).reshape((-1,) + (1,) * (len(shape) - 1 - position))
    return loudness


def gaussian(rng, dims, scale, most, cuts=(), held_as=jnp.bfloat16):
    values = scale * jax.random.normal(rng, dims, jnp.float32)
    if cuts:
        values = values * shard_levels(rng, dims, cuts, -0.22, 0.18)
    return jnp.clip(values, -most, most).astype(held_as)


def setup_inputs(seed: int = 0) -> dict:
    arg_keys = jax.random.split(jax.random.key(seed), 8)
    tokens = gaussian(arg_keys[0], (TOKENS, D), 1.0, 6.0, ((0, 16),))
    qkv_weight = gaussian(arg_keys[1], (3, D, HEADS * HEAD_DIM), D ** -0.5, 0.109375, ((2, 2),))
    query_gain = jnp.clip(1.0 + 0.18 * jax.random.normal(arg_keys[2], (HEAD_DIM,), jnp.float32), 0.1, 1.9)
    key_gain = jnp.clip(1.0 + 0.18 * jax.random.normal(arg_keys[3], (HEAD_DIM,), jnp.float32), 0.1, 1.9)
    labels = draw_labels(jax.random.fold_in(arg_keys[7], 71), 0)
    space_mask = draw_space_mask(jax.random.fold_in(arg_keys[7], 71), 0)
    time_mask = draw_time_mask(jax.random.fold_in(arg_keys[7], 71), 0)
    return dict(tokens=tokens, qkv_weight=qkv_weight, query_gain=query_gain, key_gain=key_gain, labels=labels, space_mask=space_mask, time_mask=time_mask)


epsilon = 1e-06

def normed(projected, gains):
    inverse_rms = lax.rsqrt(lax.optimization_barrier(jnp.mean(projected * projected, axis=-1, keepdims=True)) + epsilon)
    return (projected * inverse_rms * gains).astype(jnp.bfloat16)

def expand(block_mask):
    widened = jnp.repeat(block_mask.astype(jnp.float32), BLOCK, axis=-2)
    return jnp.repeat(widened, BLOCK, axis=-1)

def attend(queries, key_rows, values, allowed):
    scores = jnp.einsum('...rd,...cd->...rc', queries.astype(jnp.float32), key_rows.astype(jnp.float32)) / math.sqrt(HEAD_DIM)
    weight = jnp.exp(scores) * allowed
    denominator = lax.optimization_barrier(jnp.sum(weight, axis=-1, keepdims=True))
    rounded = lax.optimization_barrier(weight.astype(jnp.bfloat16)).astype(jnp.float32)
    return jnp.einsum('...rc,...cd->...rd', rounded, values.astype(jnp.float32)) / denominator

def space_head(queries, key_rows, values, space_live, time_live):
    blank = jnp.zeros((1, TOK_FRAME, HEAD_DIM), jnp.bfloat16)
    padded_keys = jnp.concatenate([blank, key_rows, blank], axis=0)
    padded_values = jnp.concatenate([blank, values, blank], axis=0)
    window_keys = jnp.concatenate([padded_keys[:-2], padded_keys[1:-1], padded_keys[2:]], axis=1)
    window_values = jnp.concatenate([padded_values[:-2], padded_values[1:-1], padded_values[2:]], axis=1)
    frame_ids = jnp.arange(FRAMES, dtype=jnp.int32)
    lower_ok = (frame_ids > 0).astype(jnp.float32)
    upper_ok = (frame_ids < FRAMES - 1).astype(jnp.float32)
    ones_row = jnp.ones((FRAMES, QBLOCKS), jnp.float32)
    reach = jnp.concatenate([ones_row * lower_ok[:, None], ones_row, ones_row * upper_ok[:, None]], axis=1)

    def one_frame(frame_items):
        frame_q, frame_k, frame_v, frame_reach = frame_items
        allowed = expand(space_live.astype(jnp.float32) * frame_reach[None, :])
        return attend(frame_q, frame_k, frame_v, allowed)
    return lax.map(one_frame, (queries, window_keys, window_values, reach))

def to_strips(whole):
    strip_count = TOK_FRAME // STRIP
    shaped = whole.reshape(FRAMES, strip_count, STRIP, HEAD_DIM).transpose(1, 0, 2, 3)
    return shaped.reshape(strip_count, FRAMES * STRIP, HEAD_DIM)

def time_head(queries, key_rows, values, space_live, time_live):
    strip_count = TOK_FRAME // STRIP
    allowed = expand(time_live)[None]
    result = attend(to_strips(queries), to_strips(key_rows), to_strips(values), allowed)
    result = result.reshape(strip_count, FRAMES, STRIP, HEAD_DIM).transpose(1, 0, 2, 3)
    return result.reshape(FRAMES, TOK_FRAME, HEAD_DIM)

def reference(tokens, qkv_weight, query_gain, key_gain, labels, space_mask, time_mask):

    def project(index):
        product = jnp.dot(tokens, qkv_weight[index], preferred_element_type=jnp.float32)
        return product.reshape(FRAMES, TOK_FRAME, HEADS, HEAD_DIM)
    queries = normed(project(0), query_gain).transpose(2, 0, 1, 3)
    key_rows = normed(project(1), key_gain).transpose(2, 0, 1, 3)
    values = project(2).astype(jnp.bfloat16).transpose(2, 0, 1, 3)

    def one_head(head_items):
        head_q, head_k, head_v, label, space_live, time_live = head_items
        return lax.cond(label == 1, time_head, space_head, head_q, head_k, head_v, space_live, time_live)
    mixed = lax.map(one_head, (queries, key_rows, values, labels, space_mask, time_mask))
    return mixed.transpose(1, 2, 0, 3).reshape(TOKENS, HEADS * HEAD_DIM).astype(jnp.bfloat16)
```

```python
import functools
import math

import jax
import jax.numpy as jnp
from jax import lax
from jax.experimental import pallas as pl
from jax.experimental.pallas import tpu as pltpu
from jax.sharding import PartitionSpec as P

STRIP = 8
BLOCK = 64
NEAR_MAX = 8
HD = 128
epsilon = 1e-06
BIG = 1e30
VMEM_LIMIT = 56 * 1024 * 1024


def chunk_rows(rows, want):
    while rows % want:
        want //= 2
    return want


def normed_head(projected, gains):
    inverse_rms = lax.rsqrt(jnp.mean(projected * projected, axis=-1, keepdims=True) + epsilon)
    return (projected * inverse_rms * gains).astype(jnp.bfloat16)


def project_rows(x_ref, w_refs, rows, gq, gk, put):
    x = x_ref[rows, :]
    for kind in range(3):
        w = [w_ref[kind] for w_ref in w_refs]
        w = w[0] if len(w) == 1 else jnp.concatenate(w, axis=1)
        product = jnp.dot(x, w, preferred_element_type=jnp.float32)
        for j in range(len(w_refs)):
            part = product[:, j * HD : (j + 1) * HD]
            if kind == 0:
                part = normed_head(part, gq)
            elif kind == 1:
                part = normed_head(part, gk)
            else:
                part = part.astype(jnp.bfloat16)
            put(kind, j, part)


def time_project_kernel(pair, heads, x_ref, gq_ref, gk_ref, *refs):
    w_refs, out_ref = refs[:pair], refs[pair]
    frames, _, _, pos, _ = out_ref.shape
    step = chunk_rows(x_ref.shape[0], 512)
    per = step // pos
    gq, gk = gq_ref[...], gk_ref[...]

    def body(m, carry):
        def put(kind, j, value):
            out_ref[pl.ds(m * per, per), kind, j] = value.reshape(per, pos, HD)

        project_rows(x_ref, w_refs, pl.ds(pl.multiple_of(m * step, step), step), gq, gk, put)
        return carry

    lax.fori_loop(0, x_ref.shape[0] // step, body, 0)


def time_project(tokens, weight, gq, gk, heads, frames):
    rows, d = tokens.shape
    count = heads.shape[0]
    pair = 2 if count % 2 == 0 else 1
    pos = rows // frames

    def w_spec(j):
        return pl.BlockSpec((3, d, HD), lambda i, t: (0, 0, t[pair * i + j]))

    gain = pl.BlockSpec((1, HD), lambda i, t: (0, 0))
    return pl.pallas_call(
        functools.partial(time_project_kernel, pair),
        out_shape=jax.ShapeDtypeStruct((frames, 3, count, pos, HD), jnp.bfloat16),
        grid_spec=pltpu.PrefetchScalarGridSpec(
            num_scalar_prefetch=1,
            grid=(count // pair,),
            in_specs=[
                pl.BlockSpec((rows, d), lambda i, t: (0, 0), pipeline_mode=pl.Buffered(1)),
                gain,
                gain,
            ]
            + [w_spec(j) for j in range(pair)],
            out_specs=pl.BlockSpec((frames, 3, pair, pos, HD), lambda i, t: (0, 0, i, 0, 0)),
        ),
        compiler_params=pltpu.CompilerParams(vmem_limit_bytes=VMEM_LIMIT),
        cost_estimate=pl.CostEstimate(
            flops=2 * rows * d * 3 * count * HD,
            bytes_accessed=2 * (rows * d + 3 * d * count * HD + 3 * rows * count * HD),
            transcendentals=0,
        ),
        name="time_project",
    )(heads, tokens, gq, gk, *([weight] * pair))


def space_project_kernel(pair, table, x_ref, gq_ref, gk_ref, after_ref, *refs):
    w_refs, (out_ref, next_ref, prev_ref) = refs[:pair], refs[pair:]
    i = pl.program_id(0)
    count = pl.num_programs(0) * pair
    step = chunk_rows(x_ref.shape[0], 512)
    gq, gk = gq_ref[...], gk_ref[...]

    def body(m, carry):
        rows = pl.ds(pl.multiple_of(m * step, step), step)

        def put(kind, j, value):
            out_ref[kind, j, rows, :] = value

        project_rows(x_ref, w_refs, rows, gq, gk, put)
        return carry

    lax.fori_loop(0, x_ref.shape[0] // step, body, 0)
    for j in range(pair):
        head = i * pair + j
        for s in range(NEAR_MAX):
            for side, ref in ((0, next_ref), (1, prev_ref)):
                b = table[count + (head * 2 + side) * NEAR_MAX + s]
                src = pl.ds(pl.multiple_of(b * BLOCK, BLOCK), BLOCK)
                ref[0, j, s * BLOCK : (s + 1) * BLOCK, :] = out_ref[1, j, src, :]
                ref[1, j, s * BLOCK : (s + 1) * BLOCK, :] = out_ref[2, j, src, :]


def space_project(tokens, weight, gq, gk, heads, picks, after):
    rows, d = tokens.shape
    count = heads.shape[0]
    pair = 2
    near = NEAR_MAX * BLOCK
    table = jnp.concatenate([heads, picks.reshape(-1)])

    def w_spec(j):
        return pl.BlockSpec((3, d, HD), lambda i, t: (0, 0, t[pair * i + j]))

    gain = pl.BlockSpec((1, HD), lambda i, t: (0, 0))
    near_spec = pl.BlockSpec((2, pair, near, HD), lambda i, t: (0, i, 0, 0))
    near_shape = jax.ShapeDtypeStruct((2, count, near, HD), jnp.bfloat16)
    return pl.pallas_call(
        functools.partial(space_project_kernel, pair),
        out_shape=(jax.ShapeDtypeStruct((3, count, rows, HD), jnp.bfloat16), near_shape, near_shape),
        grid_spec=pltpu.PrefetchScalarGridSpec(
            num_scalar_prefetch=1,
            grid=(count // pair,),
            in_specs=[
                pl.BlockSpec((rows, d), lambda i, t: (0, 0), pipeline_mode=pl.Buffered(1)),
                gain,
                gain,
                pl.BlockSpec(memory_space=pl.ANY),
            ]
            + [w_spec(j) for j in range(pair)],
            out_specs=(
                pl.BlockSpec((3, pair, rows, HD), lambda i, t: (0, i, 0, 0)),
                near_spec,
                near_spec,
            ),
        ),
        compiler_params=pltpu.CompilerParams(vmem_limit_bytes=VMEM_LIMIT),
        cost_estimate=pl.CostEstimate(
            flops=2 * rows * d * 3 * count * HD,
            bytes_accessed=2 * (rows * d + 3 * d * count * HD + 3 * rows * count * HD),
            transcendentals=0,
        ),
        name="space_project",
    )(table, tokens, gq, gk, after, *([weight] * pair))


def attend_rows(queries, keys, values, factor):
    scores = lax.dot_general(
        queries, keys, (((1,), (1,)), ((), ())), preferred_element_type=jnp.float32
    )
    weight = jnp.exp2(scores * factor).astype(jnp.bfloat16)
    both = jnp.dot(weight, values, preferred_element_type=jnp.float32)
    return (both[:, :HD] / both[:, HD:]).astype(jnp.bfloat16)


def space_attend_kernel(factor, parts, own_half, qkv_ref, prev_ref, next_ref, bias_ref, out_ref, ka, va, marks):
    rows = qkv_ref.shape[1]
    near = prev_ref.shape[1]
    total = rows + 2 * near

    @pl.when(pl.program_id(0) == 0)
    def _():
        va[:, HD:] = jnp.ones((total, HD), jnp.bfloat16)
        row = lax.broadcasted_iota(jnp.int32, (rows, HD), 0) // BLOCK
        lane = lax.broadcasted_iota(jnp.int32, (rows, HD), 1)
        marks[...] = jnp.where(row == lane, 1.0, 0.0).astype(jnp.bfloat16)

    for slot, ref in ((0, ka), (1, va)):
        ref[:rows, :HD] = qkv_ref[1 + slot]
        ref[rows : rows + near, :HD] = prev_ref[slot]
        ref[rows + near :, :HD] = next_ref[slot]
    for b in range(total // BLOCK):
        ka[b * BLOCK : (b + 1) * BLOCK, HD:] = jnp.broadcast_to(
            bias_ref[b : b + 1, :], (BLOCK, HD)
        ).astype(jnp.bfloat16)
    part = rows // parts
    step = chunk_rows(part, 256)
    for m in range(rows // step):
        span = slice(m * step, (m + 1) * step)
        queries = jnp.concatenate([qkv_ref[0, span, :], marks[span, :]], axis=1)
        result = attend_rows(queries, ka[...], va[...], factor)
        which = lax.rem(m * step // part - own_half[0] + parts, parts)
        first = (m * step) % part
        out_ref[which, first : first + step, :] = result


def space_attend(qkv, prev_kv, next_kv, bias, parts, shift):
    _, count, rows, _ = qkv.shape
    near = prev_kv.shape[2]
    total = rows + 2 * near
    factor = math.log2(math.e) / math.sqrt(HD)
    near_spec = pl.BlockSpec((2, None, near, HD), lambda h, t: (0, h, 0, 0))
    return pl.pallas_call(
        functools.partial(space_attend_kernel, factor, parts),
        out_shape=jax.ShapeDtypeStruct((parts, count, rows // parts, HD), jnp.bfloat16),
        grid_spec=pltpu.PrefetchScalarGridSpec(
            num_scalar_prefetch=1,
            grid=(count,),
            in_specs=[
                pl.BlockSpec((3, None, rows, HD), lambda h, t: (0, h, 0, 0)),
                near_spec,
                near_spec,
                pl.BlockSpec((None, total // BLOCK, HD), lambda h, t: (h, 0, 0)),
            ],
            out_specs=pl.BlockSpec((parts, None, rows // parts, HD), lambda h, t: (0, h, 0, 0)),
            scratch_shapes=[
                pltpu.VMEM((total, 2 * HD), jnp.bfloat16),
                pltpu.VMEM((total, 2 * HD), jnp.bfloat16),
                pltpu.VMEM((rows, HD), jnp.bfloat16),
            ],
        ),
        compiler_params=pltpu.CompilerParams(vmem_limit_bytes=VMEM_LIMIT),
        cost_estimate=pl.CostEstimate(
            flops=8 * count * rows * total * HD,
            bytes_accessed=2 * HD * count * (4 * rows + 4 * near),
            transcendentals=count * rows * total,
        ),
        name="space_attend",
    )(shift, qkv, prev_kv, next_kv, bias)


def time_attend_kernel(factor, blocks, mask, x_ref, out_ref, ka, va):
    frames, _, pos, _ = x_ref.shape
    rows = frames * pos
    span = pos * (BLOCK // STRIP)
    head = pl.program_id(0)
    ka[:, :HD] = x_ref[:, 1].reshape(rows, HD)
    va[:, :HD] = x_ref[:, 2].reshape(rows, HD)
    va[:, HD:] = jnp.ones((rows, HD), jnp.bfloat16)
    row = lax.broadcasted_iota(jnp.int32, (rows, HD), 0)
    lane = lax.broadcasted_iota(jnp.int32, (rows, HD), 1)
    strip = lax.rem(row, pos) // STRIP
    block = row // span
    lane_strip, lane_block = lane // blocks, lax.rem(lane, blocks)
    live = jnp.zeros((rows, HD), jnp.float32)
    for a in range(blocks):
        for b in range(blocks):
            m = mask[(head * blocks + a) * blocks + b].astype(jnp.float32)
            live = jnp.where((lane_block == a) & (block == b), m, live)
    live = jnp.where(strip == lane_strip, live, 0.0)
    ka[:, HD:] = ((live - 1.0) * BIG).astype(jnp.bfloat16)
    marks = jnp.where(strip * blocks + block == lane, 1.0, 0.0).astype(jnp.bfloat16)
    queries = jnp.concatenate([x_ref[:, 0].reshape(rows, HD), marks], axis=1)
    step = chunk_rows(rows, 256)
    per = step // pos
    for m in range(rows // step):
        result = attend_rows(queries[m * step : (m + 1) * step], ka[...], va[...], factor)
        out_ref[m * per : (m + 1) * per] = result.reshape(per, pos, HD)


def time_attend(received, mask):
    frames, _, count, pos, _ = received.shape
    rows = frames * pos
    factor = math.log2(math.e) / math.sqrt(HD)
    return pl.pallas_call(
        functools.partial(time_attend_kernel, factor, mask.shape[1]),
        out_shape=jax.ShapeDtypeStruct((frames, count, pos, HD), jnp.bfloat16),
        grid_spec=pltpu.PrefetchScalarGridSpec(
            num_scalar_prefetch=1,
            grid=(count,),
            in_specs=[pl.BlockSpec((frames, 3, None, pos, HD), lambda h, t: (0, 0, h, 0, 0))],
            out_specs=pl.BlockSpec((frames, None, pos, HD), lambda h, t: (0, h, 0, 0)),
            scratch_shapes=[
                pltpu.VMEM((rows, 2 * HD), jnp.bfloat16),
                pltpu.VMEM((rows, 2 * HD), jnp.bfloat16),
            ],
        ),
        compiler_params=pltpu.CompilerParams(vmem_limit_bytes=VMEM_LIMIT),
        cost_estimate=pl.CostEstimate(
            flops=8 * count * rows * rows * HD,
            bytes_accessed=8 * HD * count * rows,
            transcendentals=count * rows * rows,
        ),
        name="time_attend",
    )(mask.reshape(-1), received)


def assemble_kernel(table, sk_ref, sr_ref, tk_ref, tr_ref, out_ref):
    g = pl.program_id(0)
    groups = pl.num_programs(0)
    slot = table[g]
    other = table[groups + g]
    rows = out_ref.shape[0]

    def write(s_ref, t_ref):
        first, second = s_ref[0], s_ref[1]
        timed = t_ref[...].reshape(rows, HD)
        for want in range(3):

            @pl.when(slot == want)
            def _():
                order = [first, second]
                order.insert(want, timed)
                for c in range(3):
                    out_ref[:, c * HD : (c + 1) * HD] = order[c]

    @pl.when(other == 0)
    def _():
        write(sk_ref, tk_ref)

    @pl.when(other == 1)
    def _():
        write(sr_ref, tr_ref)


def assemble(slots, other, space_at, time_side, group_at, space_keep, space_recv, time_keep, time_recv, chunks):
    groups = slots.shape[0]
    rows = space_keep.shape[1]
    pos = time_keep.shape[2]
    table = jnp.concatenate([slots, other, space_at, time_side, group_at])
    space_spec = pl.BlockSpec((2, rows, HD), lambda g, t: (t[2 * groups + g], 0, 0))
    time_spec = pl.BlockSpec(
        (chunks, None, pos, HD), lambda g, t: (t[3 * groups + g], t[4 * groups + g], 0, 0)
    )
    return pl.pallas_call(
        assemble_kernel,
        out_shape=jax.ShapeDtypeStruct((rows, groups * 3 * HD), jnp.bfloat16),
        grid_spec=pltpu.PrefetchScalarGridSpec(
            num_scalar_prefetch=1,
            grid=(groups,),
            in_specs=[space_spec, space_spec, time_spec, time_spec],
            out_specs=pl.BlockSpec((rows, 3 * HD), lambda g, t: (0, g)),
        ),
        cost_estimate=pl.CostEstimate(
            flops=0, bytes_accessed=8 * rows * groups * 3 * HD, transcendentals=0
        ),
        name="assemble",
    )(table, space_keep, space_recv, time_keep, time_recv)


def block_picks(live):
    used = jnp.max(live, axis=1)
    width = used.shape[1]
    before = (jnp.arange(width)[:, None] < jnp.arange(width)[None, :]).astype(jnp.int32)
    rank = jnp.sum(used[:, :, None] * before[None], axis=1)
    return used[:, None, :] * (rank[:, None, :] == jnp.arange(NEAR_MAX)[None, :, None]).astype(jnp.int32)


def on_device(tokens, qkv_weight, query_gain, key_gain, labels, space_mask, time_mask):
    frame_count = lax.axis_size("frame")
    sides = lax.axis_size("head")
    own_frame = lax.axis_index("frame")
    own_side = lax.axis_index("head")
    row_count = tokens.shape[0]
    groups = labels.shape[0] // 3
    blocks = row_count // BLOCK
    space_count = 2 * groups
    gq, gk = query_gain.reshape(1, HD), key_gain.reshape(1, HD)

    picked = labels.reshape(groups, 3)
    time_slot = jnp.sum(picked * jnp.arange(3, dtype=jnp.int32)[None, :], axis=1)
    group_base = 3 * jnp.arange(groups, dtype=jnp.int32)
    time_heads = group_base + time_slot
    first_space = group_base + jnp.where(time_slot == 0, 1, 0)
    second_space = group_base + jnp.where(time_slot == 2, 1, 2)
    space_heads = jnp.stack([first_space, second_space], axis=1).reshape(space_count)

    packed = time_project(tokens, qkv_weight, gq, gk, time_heads, frame_count)
    received = lax.all_to_all(packed, "frame", split_axis=0, concat_axis=0, tiled=True)

    live = jnp.take(space_mask, space_heads, axis=0)
    low, own, high = live[:, :, :blocks], live[:, :, blocks : 2 * blocks], live[:, :, 2 * blocks :]
    low_pick, high_pick = block_picks(low), block_picks(high)
    ids = jnp.arange(blocks, dtype=jnp.int32)
    picks = jnp.stack([jnp.sum(low_pick * ids, axis=-1), jnp.sum(high_pick * ids, axis=-1)], axis=1)
    low_ok = (own_frame > 0).astype(jnp.int32)
    high_ok = (own_frame < frame_count - 1).astype(jnp.int32)

    def near_live(pick, side, ok):
        return ok * jnp.sum(pick[:, :, None, :] * side[:, None, :, :], axis=-1)

    allowed = jnp.concatenate(
        [jnp.swapaxes(own, 1, 2), near_live(low_pick, low, low_ok), near_live(high_pick, high, high_ok)],
        axis=1,
    )
    bias = jnp.pad((allowed.astype(jnp.float32) - 1.0) * BIG, ((0, 0), (0, 0), (0, HD - blocks)))

    qkv, to_next, to_prev = space_project(tokens, qkv_weight, gq, gk, space_heads, picks, packed)
    up = [(i, i + 1) for i in range(frame_count - 1)]
    down = [(i + 1, i) for i in range(frame_count - 1)]
    prev_kv = lax.ppermute(to_next, "frame", up)
    next_kv = lax.ppermute(to_prev, "frame", down)

    shift = own_side if sides == 2 else jnp.int32(0)
    space_out = space_attend(
        qkv, prev_kv, next_kv, bias, sides, jnp.reshape(shift, (1,)).astype(jnp.int32)
    )
    time_out = time_attend(received, jnp.take(time_mask, time_heads, axis=0))
    returned = lax.all_to_all(time_out, "frame", split_axis=0, concat_axis=0, tiled=True)

    part_rows = row_count // sides
    chunks = frame_count // sides
    side_ids = jnp.repeat(jnp.arange(sides, dtype=jnp.int32), groups)
    group_ids = jnp.tile(jnp.arange(groups, dtype=jnp.int32), sides)
    zeros = jnp.zeros_like(side_ids)
    if sides == 2:
        swap = [(0, 1), (1, 0)]
        their_slot = lax.ppermute(time_slot, "head", swap)
        slots = jnp.where(
            own_side == 0,
            jnp.concatenate([time_slot, their_slot]),
            jnp.concatenate([their_slot, time_slot]),
        )
        space_keep = space_out[0]
        space_recv = lax.ppermute(space_out[1], "head", swap)
        time_keep = lax.dynamic_slice_in_dim(returned, own_side * chunks, chunks, 0)
        time_recv = lax.ppermute(
            lax.dynamic_slice_in_dim(returned, (1 - own_side) * chunks, chunks, 0), "head", swap
        )
        other = (side_ids != own_side).astype(jnp.int32)
        space_at, time_side = group_ids, zeros
    else:
        slots = lax.all_to_all(
            jnp.broadcast_to(time_slot[None], (sides, groups)), "head", 0, 0, tiled=True
        ).reshape(-1)
        space_keep = lax.all_to_all(space_out, "head", 0, 0, tiled=True)
        space_keep = space_keep.reshape(sides * space_count, part_rows, HD)
        space_recv = space_keep
        time_keep = lax.all_to_all(returned, "head", 0, 0, tiled=True)
        time_recv = time_keep
        other, space_at, time_side = zeros, side_ids * groups + group_ids, side_ids
    return assemble(
        slots, other, space_at, time_side, group_ids, space_keep, space_recv, time_keep, time_recv, chunks
    )


def solution(mesh):
    placed = (
        P("frame", None),
        P(None, None, "head"),
        P(),
        P(),
        P("head"),
        P("head", None, None),
        P("head", None, None),
    )
    return jax.shard_map(
        on_device, mesh=mesh, in_specs=placed, out_specs=P(("frame", "head"), None), check_vma=False
    )
```

```python
import functools
import math

import jax
import jax.numpy as jnp
from jax import lax
from jax.experimental import pallas as pl
from jax.experimental.pallas import tpu as pltpu
from jax.sharding import PartitionSpec as P


STRIP = 8
BLOCK = 64
NEAR_MAX = 8
HD = 128
epsilon = 1e-06
BIG = 1e30
VMEM_LIMIT = 56 * 1024 * 1024


def chunk_rows(rows, want):
    while rows % want:
        want //= 2
    return want


def normed_head(projected, gains):
    inverse_rms = lax.rsqrt(jnp.mean(projected * projected, axis=-1, keepdims=True) + epsilon)
    return (projected * inverse_rms * gains).astype(jnp.bfloat16)


def project_kernel(kinds, pair, near_count, strips, table, x_ref, gq_ref, gk_ref, after_ref, *refs):
    weights = refs[: len(kinds) * pair]
    outs = refs[len(kinds) * pair :]
    out_ref = outs[0]
    i = pl.program_id(0)
    count = pl.num_programs(0) * pair
    step = chunk_rows(x_ref.shape[0], 512)
    gains = {0: gq_ref[...], 1: gk_ref[...]}

    def body(m, carry):
        rows = pl.ds(pl.multiple_of(m * step, step), step)
        x = x_ref[rows, :]
        for n, kind in enumerate(kinds):
            w = [w_ref[...] for w_ref in weights[n * pair : (n + 1) * pair]]
            w = w[0] if pair == 1 else jnp.concatenate(w, axis=1)
            product = jnp.dot(x, w, preferred_element_type=jnp.float32)
            for j in range(pair):
                part = product[:, j * HD : (j + 1) * HD]
                if kind in gains:
                    part = normed_head(part, gains[kind])
                else:
                    part = part.astype(jnp.bfloat16)
                if strips:
                    pos = out_ref.shape[3]
                    per = step // pos
                    out_ref[pl.ds(m * per, per), n, j] = part.reshape(per, pos, HD)
                else:
                    out_ref[n, j, rows, :] = part
        return carry

    lax.fori_loop(0, x_ref.shape[0] // step, body, 0)
    for j in range(pair if near_count else 0):
        head = i * pair + j
        for s in range(near_count):
            for side, ref in ((0, outs[1]), (1, outs[2])):
                b = table[count + (head * 2 + side) * near_count + s]
                src = pl.ds(pl.multiple_of(b * BLOCK, BLOCK), BLOCK)
                for n in range(2):
                    ref[n, j, s * BLOCK : (s + 1) * BLOCK, :] = out_ref[n, j, src, :]


def project(tokens, weight, gq, gk, heads, kinds, after, strips=0, picks=None):
    rows, d = tokens.shape
    count = heads.shape[0]
    pair = 2 if count % 2 == 0 else 1
    n = len(kinds)
    near_count = 0 if picks is None else NEAR_MAX
    table = heads if picks is None else jnp.concatenate([heads, picks.reshape(-1)])

    def w_spec(kind, j):
        return pl.BlockSpec((None, d, HD), lambda i, t: (kind, 0, t[pair * i + j]))

    gain = pl.BlockSpec((1, HD), lambda i, t: (0, 0))
    if strips:
        pos = rows // strips
        shapes = [jax.ShapeDtypeStruct((strips, n, count, pos, HD), jnp.bfloat16)]
        specs = [pl.BlockSpec((strips, n, pair, pos, HD), lambda i, t: (0, 0, i, 0, 0))]
    else:
        shapes = [jax.ShapeDtypeStruct((n, count, rows, HD), jnp.bfloat16)]
        specs = [pl.BlockSpec((n, pair, rows, HD), lambda i, t: (0, i, 0, 0))]
    if near_count:
        near = near_count * BLOCK
        shapes += [jax.ShapeDtypeStruct((2, count, near, HD), jnp.bfloat16)] * 2
        specs += [pl.BlockSpec((2, pair, near, HD), lambda i, t: (0, i, 0, 0))] * 2
    out = pl.pallas_call(
        functools.partial(project_kernel, kinds, pair, near_count, bool(strips)),
        out_shape=tuple(shapes),
        grid_spec=pltpu.PrefetchScalarGridSpec(
            num_scalar_prefetch=1,
            grid=(count // pair,),
            in_specs=[
                pl.BlockSpec((rows, d), lambda i, t: (0, 0), pipeline_mode=pl.Buffered(1)),
                gain,
                gain,
                pl.BlockSpec(memory_space=pl.ANY),
            ]
            + [w_spec(kind, j) for kind in kinds for j in range(pair)],
            out_specs=tuple(specs),
        ),
        compiler_params=pltpu.CompilerParams(vmem_limit_bytes=VMEM_LIMIT),
        cost_estimate=pl.CostEstimate(
            flops=2 * rows * d * n * count * HD,
            bytes_accessed=2 * (rows * d + n * d * count * HD + n * rows * count * HD),
            transcendentals=0,
        ),
    )(table, tokens, gq, gk, after, *([weight] * (n * pair)))
    return out if near_count else out[0]


def attend_rows(queries, keys, values, factor):
    scores = lax.dot_general(
        queries, keys, (((1,), (1,)), ((), ())), preferred_element_type=jnp.float32
    )
    weight = jnp.exp2(scores * factor).astype(jnp.bfloat16)
    both = jnp.dot(weight, values, preferred_element_type=jnp.float32)
    return (both[:, :HD] / both[:, HD:]).astype(jnp.bfloat16)


def space_attend_kernel(factor, parts, side, q_ref, kv_ref, prev_ref, next_ref, bias_ref, after_ref, *refs):
    outs, (ka, va, marks) = refs[:-3], refs[-3:]
    rows = q_ref.shape[0]
    near = prev_ref.shape[1]
    total = rows + 2 * near

    @pl.when(pl.program_id(0) == 0)
    def _():
        va[:, HD:] = jnp.ones((total, HD), jnp.bfloat16)
        row = lax.broadcasted_iota(jnp.int32, (rows, HD), 0) // BLOCK
        lane = lax.broadcasted_iota(jnp.int32, (rows, HD), 1)
        marks[...] = jnp.where(row == lane, 1.0, 0.0).astype(jnp.bfloat16)

    for slot, ref in ((0, ka), (1, va)):
        ref[:rows, :HD] = kv_ref[slot]
        ref[rows : rows + near, :HD] = prev_ref[slot]
        ref[rows + near :, :HD] = next_ref[slot]
    for b in range(total // BLOCK):
        ka[b * BLOCK : (b + 1) * BLOCK, HD:] = jnp.broadcast_to(
            bias_ref[b : b + 1, :], (BLOCK, HD)
        ).astype(jnp.bfloat16)
    part = rows // parts
    step = chunk_rows(part, 256)
    for m in range(rows // step):
        span = slice(m * step, (m + 1) * step)
        queries = jnp.concatenate([q_ref[span, :], marks[span, :]], axis=1)
        result = attend_rows(queries, ka[...], va[...], factor)
        half = m * step // part
        rest = slice(m * step % part, m * step % part + step)
        if len(outs) == 1:
            outs[0][half, rest, :] = result
        else:

            @pl.when(side[0] == half)
            def _():
                outs[0][rest, :] = result

            @pl.when(side[0] != half)
            def _():
                outs[1][rest, :] = result


def space_attend(q, kv, prev_kv, next_kv, bias, first, count, parts, side, after):
    rows = q.shape[2]
    near = prev_kv.shape[2]
    total = rows + 2 * near
    factor = math.log2(math.e) / math.sqrt(HD)
    near_spec = pl.BlockSpec((2, None, near, HD), lambda h, t: (0, first + h, 0, 0))
    part = rows // parts
    if parts == 2:
        shapes = [jax.ShapeDtypeStruct((count, part, HD), jnp.bfloat16)] * 2
        specs = [pl.BlockSpec((None, part, HD), lambda h, t: (h, 0, 0))] * 2
    else:
        shapes = [jax.ShapeDtypeStruct((parts, count, part, HD), jnp.bfloat16)]
        specs = [pl.BlockSpec((parts, None, part, HD), lambda h, t: (0, h, 0, 0))]
    return pl.pallas_call(
        functools.partial(space_attend_kernel, factor, parts),
        out_shape=tuple(shapes),
        grid_spec=pltpu.PrefetchScalarGridSpec(
            num_scalar_prefetch=1,
            grid=(count,),
            in_specs=[
                pl.BlockSpec((None, None, rows, HD), lambda h, t: (0, first + h, 0, 0)),
                pl.BlockSpec((2, None, rows, HD), lambda h, t: (0, first + h, 0, 0)),
                near_spec,
                near_spec,
                pl.BlockSpec((None, total // BLOCK, HD), lambda h, t: (first + h, 0, 0)),
                pl.BlockSpec(memory_space=pl.ANY),
            ],
            out_specs=tuple(specs),
            scratch_shapes=[
                pltpu.VMEM((total, 2 * HD), jnp.bfloat16),
                pltpu.VMEM((total, 2 * HD), jnp.bfloat16),
                pltpu.VMEM((rows, HD), jnp.bfloat16),
            ],
        ),
        compiler_params=pltpu.CompilerParams(vmem_limit_bytes=VMEM_LIMIT),
        cost_estimate=pl.CostEstimate(
            flops=8 * count * rows * total * HD,
            bytes_accessed=2 * HD * count * (4 * rows + 4 * near),
            transcendentals=count * rows * total,
        ),
    )(side, q, kv, prev_kv, next_kv, bias, after)


def time_attend_kernel(factor, blocks, mask, x_ref, after_ref, out_ref, ka, va):
    frames, _, pos, _ = x_ref.shape
    rows = frames * pos
    span = pos * (BLOCK // STRIP)
    head = pl.program_id(0)
    ka[:, :HD] = x_ref[:, 1].reshape(rows, HD)
    va[:, :HD] = x_ref[:, 2].reshape(rows, HD)
    va[:, HD:] = jnp.ones((rows, HD), jnp.bfloat16)
    row = lax.broadcasted_iota(jnp.int32, (rows, HD), 0)
    lane = lax.broadcasted_iota(jnp.int32, (rows, HD), 1)
    strip = lax.rem(row, pos) // STRIP
    block = row // span
    lane_strip, lane_block = lane // blocks, lax.rem(lane, blocks)
    live = jnp.zeros((rows, HD), jnp.float32)
    for a in range(blocks):
        for b in range(blocks):
            m = mask[(head * blocks + a) * blocks + b].astype(jnp.float32)
            live = jnp.where((lane_block == a) & (block == b), m, live)
    live = jnp.where(strip == lane_strip, live, 0.0)
    ka[:, HD:] = ((live - 1.0) * BIG).astype(jnp.bfloat16)
    marks = jnp.where(strip * blocks + block == lane, 1.0, 0.0).astype(jnp.bfloat16)
    queries = jnp.concatenate([x_ref[:, 0].reshape(rows, HD), marks], axis=1)
    step = chunk_rows(rows, 256)
    per = step // pos
    for m in range(rows // step):
        result = attend_rows(queries[m * step : (m + 1) * step], ka[...], va[...], factor)
        out_ref[m * per : (m + 1) * per] = result.reshape(per, pos, HD)


def time_attend(received, mask, after):
    frames, _, count, pos, _ = received.shape
    rows = frames * pos
    factor = math.log2(math.e) / math.sqrt(HD)
    return pl.pallas_call(
        functools.partial(time_attend_kernel, factor, mask.shape[1]),
        out_shape=jax.ShapeDtypeStruct((frames, count, pos, HD), jnp.bfloat16),
        grid_spec=pltpu.PrefetchScalarGridSpec(
            num_scalar_prefetch=1,
            grid=(count,),
            in_specs=[
                pl.BlockSpec((frames, 3, None, pos, HD), lambda h, t: (0, 0, h, 0, 0)),
                pl.BlockSpec(memory_space=pl.ANY),
            ],
            out_specs=pl.BlockSpec((frames, None, pos, HD), lambda h, t: (0, h, 0, 0)),
            scratch_shapes=[
                pltpu.VMEM((rows, 2 * HD), jnp.bfloat16),
                pltpu.VMEM((rows, 2 * HD), jnp.bfloat16),
            ],
        ),
        compiler_params=pltpu.CompilerParams(vmem_limit_bytes=VMEM_LIMIT),
        cost_estimate=pl.CostEstimate(
            flops=8 * count * rows * rows * HD,
            bytes_accessed=8 * HD * count * rows,
            transcendentals=count * rows * rows,
        ),
        name="time_attend",
    )(mask.reshape(-1), received, after)


def assemble_kernel(sources, table, *refs):
    g = pl.program_id(0)
    groups = pl.num_programs(0)
    out_ref = refs[-1]
    slot, chosen = table[g], table[groups + g]
    rows = out_ref.shape[0]
    for n in range(sources):
        s_ref, t_ref = refs[2 * n], refs[2 * n + 1]
        for want in range(3):

            @pl.when((chosen == n) & (slot == want))
            def _():
                order = [s_ref[0], s_ref[1]]
                order.insert(want, t_ref[...].reshape(rows, HD))
                for c in range(3):
                    out_ref[:, c * HD : (c + 1) * HD] = order[c]


def assemble(slots, chosen, sources, chunks):
    groups = slots.shape[0]
    rows = sources[0][0].shape[1]
    tables, specs, arrays = [slots, chosen], [], []
    for n, (space, timed, side, at) in enumerate(sources):
        per = timed.shape[1]
        pos = timed.shape[2]
        tables += [side, at]

        def space_index(g, t, n=n, per=per):
            return (t[(2 + 2 * n) * groups + g] * per + t[(3 + 2 * n) * groups + g], 0, 0)

        def time_index(g, t, n=n):
            return (t[(2 + 2 * n) * groups + g], t[(3 + 2 * n) * groups + g], 0, 0)

        specs += [pl.BlockSpec((2, rows, HD), space_index), pl.BlockSpec((chunks, None, pos, HD), time_index)]
        arrays += [space, timed]
    return pl.pallas_call(
        functools.partial(assemble_kernel, len(sources)),
        out_shape=jax.ShapeDtypeStruct((rows, groups * 3 * HD), jnp.bfloat16),
        grid_spec=pltpu.PrefetchScalarGridSpec(
            num_scalar_prefetch=1,
            grid=(groups,),
            in_specs=specs,
            out_specs=pl.BlockSpec((rows, 3 * HD), lambda g, t: (0, g)),
        ),
        cost_estimate=pl.CostEstimate(
            flops=0, bytes_accessed=4 * rows * groups * 3 * HD, transcendentals=0
        ),
        name="assemble",
    )(jnp.concatenate(tables), *arrays)


def block_picks(live):
    used = jnp.max(live, axis=1)
    width = used.shape[1]
    before = (jnp.arange(width)[:, None] < jnp.arange(width)[None, :]).astype(jnp.int32)
    rank = jnp.sum(used[:, :, None] * before[None], axis=1)
    return used[:, None, :] * (rank[:, None, :] == jnp.arange(NEAR_MAX)[None, :, None]).astype(jnp.int32)


def on_device(tokens, qkv_weight, query_gain, key_gain, labels, space_mask, time_mask):
    frame_count = lax.axis_size("frame")
    sides = lax.axis_size("head")
    own_frame = lax.axis_index("frame")
    own_side = lax.axis_index("head")
    row_count = tokens.shape[0]
    groups = labels.shape[0] // 3
    blocks = row_count // BLOCK
    space_count = 2 * groups
    gq, gk = query_gain.reshape(1, HD), key_gain.reshape(1, HD)

    picked = labels.reshape(groups, 3)
    time_slot = jnp.sum(picked * jnp.arange(3, dtype=jnp.int32)[None, :], axis=1)
    group_base = 3 * jnp.arange(groups, dtype=jnp.int32)
    time_heads = group_base + time_slot
    first_space = group_base + jnp.where(time_slot == 0, 1, 0)
    second_space = group_base + jnp.where(time_slot == 2, 1, 2)
    space_heads = jnp.stack([first_space, second_space], axis=1).reshape(space_count)

    live = jnp.take(space_mask, space_heads, axis=0)
    low, own, high = live[:, :, :blocks], live[:, :, blocks : 2 * blocks], live[:, :, 2 * blocks :]
    low_pick, high_pick = block_picks(low), block_picks(high)
    ids = jnp.arange(blocks, dtype=jnp.int32)
    picks = jnp.stack([jnp.sum(low_pick * ids, axis=-1), jnp.sum(high_pick * ids, axis=-1)], axis=1)
    low_ok = (own_frame > 0).astype(jnp.int32)
    high_ok = (own_frame < frame_count - 1).astype(jnp.int32)

    def near_live(pick, side, ok):
        return ok * jnp.sum(pick[:, :, None, :] * side[:, None, :, :], axis=-1)

    allowed = jnp.concatenate(
        [jnp.swapaxes(own, 1, 2), near_live(low_pick, low, low_ok), near_live(high_pick, high, high_ok)],
        axis=1,
    )
    bias = jnp.pad((allowed.astype(jnp.float32) - 1.0) * BIG, ((0, 0), (0, 0), (0, HD - blocks)))

    swap = [(0, 1), (1, 0)]
    if sides == 2:
        their_slot = lax.ppermute(time_slot, "head", swap)
        picks, their_slot = lax.optimization_barrier((picks, their_slot))

    splits = 2 if groups % 2 == 0 else 1
    share = groups // splits
    up = [(i, i + 1) for i in range(frame_count - 1)]
    down = [(i + 1, i) for i in range(frame_count - 1)]
    received = []
    after = gq
    for n in range(splits):
        packed = project(
            tokens, qkv_weight, gq, gk, time_heads[n * share : (n + 1) * share], (0, 1, 2), after,
            strips=frame_count,
        )
        received.append(lax.all_to_all(packed, "frame", split_axis=0, concat_axis=0, tiled=True))
        after = packed
        if n == 0:
            kv, to_next, to_prev = project(
                tokens, qkv_weight, gq, gk, space_heads, (1, 2), after, picks=picks
            )
            prev_kv = lax.ppermute(to_next, "frame", up)
            next_kv = lax.ppermute(to_prev, "frame", down)
            after = kv
    space_q = project(tokens, qkv_weight, gq, gk, space_heads, (0,), after)

    mask = jnp.take(time_mask, time_heads, axis=0)
    side = jnp.reshape(own_side, (1,)).astype(jnp.int32)
    part_rows = row_count // sides
    chunks = frame_count // sides
    after = space_q
    returned, space_out = [], []

    def timed(n, after):
        out = time_attend(received[n], mask[n * share : (n + 1) * share], after)
        returned.append(lax.all_to_all(out, "frame", split_axis=0, concat_axis=0, tiled=True))
        return out

    if splits == 2:
        after = timed(0, after)
    for n in range(splits):
        out = space_attend(
            space_q, kv, prev_kv, next_kv, bias, n * 2 * share, 2 * share, sides, side, after
        )
        space_out.append(out)
        after = out[0]
    timed(splits - 1, after)

    side_ids = jnp.repeat(jnp.arange(sides, dtype=jnp.int32), groups)
    group_ids = jnp.tile(jnp.arange(groups, dtype=jnp.int32), sides)
    all_ids = jnp.arange(sides * groups, dtype=jnp.int32)
    zeros = jnp.zeros_like(side_ids)
    sources = []
    if sides == 2:
        slots = jnp.where(
            own_side == 0,
            jnp.concatenate([time_slot, their_slot]),
            jnp.concatenate([their_slot, time_slot]),
        )
        for n in range(splits):
            keep, send = space_out[n]
            recv = lax.ppermute(send, "head", swap)
            time_keep = lax.dynamic_slice_in_dim(returned[n], own_side * chunks, chunks, 0)
            time_send = lax.dynamic_slice_in_dim(returned[n], (1 - own_side) * chunks, chunks, 0)
            time_recv = lax.ppermute(time_send, "head", swap)
            for whose, space_part, time_part in ((own_side, keep, time_keep), (1 - own_side, recv, time_recv)):
                at = jnp.clip(all_ids - whose * groups - n * share, 0, share - 1)
                sources.append((space_part, time_part, zeros, at))
        chosen = group_ids // share * 2 + (side_ids != own_side).astype(jnp.int32)
    else:
        slots = lax.all_to_all(
            jnp.broadcast_to(time_slot[None], (sides, groups)), "head", 0, 0, tiled=True
        ).reshape(-1)
        for n in range(splits):
            space_part = lax.all_to_all(space_out[n][0], "head", 0, 0, tiled=True)
            time_part = lax.all_to_all(returned[n], "head", 0, 0, tiled=True)
            at = jnp.clip(group_ids - n * share, 0, share - 1)
            sources.append((space_part.reshape(-1, part_rows, HD), time_part, side_ids, at))
        chosen = group_ids // share
    return assemble(slots, chosen, sources, chunks)


def solution(mesh):
    placed = (
        P("frame", None),
        P(None, None, "head"),
        P(),
        P(),
        P("head"),
        P("head", None, None),
        P("head", None, None),
    )

    return jax.shard_map(
        on_device, mesh=mesh, in_specs=placed, out_specs=P(("frame", "head"), None), check_vma=False
    )
```

```python
import functools
import math

import jax
import jax.numpy as jnp
from jax import lax
from jax.experimental import pallas as pl
from jax.experimental.pallas import tpu as pltpu
from jax.sharding import PartitionSpec as P


STRIP = 8
BLOCK = 64
NEAR_MAX = 8
HD = 128
epsilon = 1e-06
BIG = 1e30
VMEM_LIMIT = 56 * 1024 * 1024


def chunk_rows(rows, want):
    while rows % want:
        want //= 2
    return want


def normed_head(projected, gains):
    inverse_rms = lax.rsqrt(jnp.mean(projected * projected, axis=-1, keepdims=True) + epsilon)
    return (projected * inverse_rms * gains).astype(jnp.bfloat16)


def project_kernel(kinds, pair, near_count, strips, table, x_ref, gq_ref, gk_ref, after_ref, *refs):
    weights = refs[: len(kinds) * pair]
    outs = refs[len(kinds) * pair :]
    out_ref = outs[0]
    i = pl.program_id(0)
    count = pl.num_programs(0) * pair
    step = x_ref.shape[0] // strips if strips > 1 else chunk_rows(x_ref.shape[0], 512)
    gains = {0: gq_ref[...], 1: gk_ref[...]}

    def body(m, carry):
        rows = pl.ds(pl.multiple_of(m * step, step), step)
        x = x_ref[rows, :]
        for n, kind in enumerate(kinds):
            w = [w_ref[...] for w_ref in weights[n * pair : (n + 1) * pair]]
            w = w[0] if pair == 1 else jnp.concatenate(w, axis=1)
            product = jnp.dot(x, w, preferred_element_type=jnp.float32)
            for j in range(pair):
                part = product[:, j * HD : (j + 1) * HD]
                if kind in gains:
                    part = normed_head(part, gains[kind])
                else:
                    part = part.astype(jnp.bfloat16)
                if strips:
                    pos = out_ref.shape[3]
                    if strips == 1:
                        per = step // pos
                        out_ref[pl.ds(m * per, per), n, j] = part.reshape(per, pos, HD)
                    else:
                        q = pos // strips
                        at = pl.ds(pl.multiple_of(m * q, q), q)
                        out_ref[:, n, j, at, :] = part.reshape(out_ref.shape[0], q, HD)
                else:
                    out_ref[n, j, rows, :] = part
        return carry

    lax.fori_loop(0, x_ref.shape[0] // step, body, 0)
    for j in range(pair if near_count else 0):
        head = i * pair + j
        for s in range(near_count):
            for side, ref in ((0, outs[1]), (1, outs[2])):
                b = table[count + (head * 2 + side) * near_count + s]
                src = pl.ds(pl.multiple_of(b * BLOCK, BLOCK), BLOCK)
                for n in range(2):
                    ref[n, j, s * BLOCK : (s + 1) * BLOCK, :] = out_ref[n, j, src, :]


def project(tokens, weight, gq, gk, heads, kinds, after, strips=0, deal=1, picks=None):
    rows, d = tokens.shape
    count = heads.shape[0]
    pair = 2 if count % 2 == 0 else 1
    n = len(kinds)
    near_count = 0 if picks is None else NEAR_MAX
    table = heads if picks is None else jnp.concatenate([heads, picks.reshape(-1)])

    def w_spec(kind, j):
        return pl.BlockSpec((None, d, HD), lambda i, t: (kind, 0, t[pair * i + j]))

    gain = pl.BlockSpec((1, HD), lambda i, t: (0, 0))
    if strips:
        pos = rows // strips
        shapes = [jax.ShapeDtypeStruct((strips, n, count, pos, HD), jnp.bfloat16)]
        specs = [pl.BlockSpec((strips, n, pair, pos, HD), lambda i, t: (0, 0, i, 0, 0))]
    else:
        shapes = [jax.ShapeDtypeStruct((n, count, rows, HD), jnp.bfloat16)]
        specs = [pl.BlockSpec((n, pair, rows, HD), lambda i, t: (0, i, 0, 0))]
    if near_count:
        near = near_count * BLOCK
        shapes += [jax.ShapeDtypeStruct((2, count, near, HD), jnp.bfloat16)] * 2
        specs += [pl.BlockSpec((2, pair, near, HD), lambda i, t: (0, i, 0, 0))] * 2
    out = pl.pallas_call(
        functools.partial(project_kernel, kinds, pair, near_count, deal if strips else 0),
        out_shape=tuple(shapes),
        grid_spec=pltpu.PrefetchScalarGridSpec(
            num_scalar_prefetch=1,
            grid=(count // pair,),
            in_specs=[
                pl.BlockSpec((rows, d), lambda i, t: (0, 0), pipeline_mode=pl.Buffered(1)),
                gain,
                gain,
                pl.BlockSpec(memory_space=pl.ANY),
            ]
            + [w_spec(kind, j) for kind in kinds for j in range(pair)],
            out_specs=tuple(specs),
        ),
        compiler_params=pltpu.CompilerParams(vmem_limit_bytes=VMEM_LIMIT),
        cost_estimate=pl.CostEstimate(
            flops=2 * rows * d * n * count * HD,
            bytes_accessed=2 * (rows * d + n * d * count * HD + n * rows * count * HD),
            transcendentals=0,
        ),
    )(table, tokens, gq, gk, after, *([weight] * (n * pair)))
    return out if near_count else out[0]


def attend_rows(queries, keys, values, factor):
    scores = lax.dot_general(
        queries, keys, (((1,), (1,)), ((), ())), preferred_element_type=jnp.float32
    )
    weight = jnp.exp2(scores * factor).astype(jnp.bfloat16)
    both = jnp.dot(weight, values, preferred_element_type=jnp.float32)
    return (both[:, :HD] / both[:, HD:]).astype(jnp.bfloat16)


def space_attend_kernel(factor, parts, side, q_ref, kv_ref, prev_ref, next_ref, bias_ref, after_ref, out_ref, ka, va, marks):
    rows = q_ref.shape[0]
    near = prev_ref.shape[1]
    total = rows + 2 * near

    @pl.when(pl.program_id(0) == 0)
    def _():
        va[:, HD:] = jnp.ones((total, HD), jnp.bfloat16)
        row = lax.broadcasted_iota(jnp.int32, (rows, HD), 0) // BLOCK
        lane = lax.broadcasted_iota(jnp.int32, (rows, HD), 1)
        marks[...] = jnp.where(row == lane, 1.0, 0.0).astype(jnp.bfloat16)

    for slot, ref in ((0, ka), (1, va)):
        ref[:rows, :HD] = kv_ref[slot]
        ref[rows : rows + near, :HD] = prev_ref[slot]
        ref[rows + near :, :HD] = next_ref[slot]
    for b in range(total // BLOCK):
        ka[b * BLOCK : (b + 1) * BLOCK, HD:] = jnp.broadcast_to(
            bias_ref[b : b + 1, :], (BLOCK, HD)
        ).astype(jnp.bfloat16)
    part = rows // parts
    step = chunk_rows(part, 256)
    for m in range(rows // step):
        span = slice(m * step, (m + 1) * step)
        queries = jnp.concatenate([q_ref[span, :], marks[span, :]], axis=1)
        result = attend_rows(queries, ka[...], va[...], factor)
        which = lax.rem(m * step // part - side[0] + parts, parts)
        first = m * step % part
        out_ref[which, first : first + step, :] = result


def space_attend(q, kv, prev_kv, next_kv, bias, parts, side, after):
    count = q.shape[1]
    rows = q.shape[2]
    near = prev_kv.shape[2]
    total = rows + 2 * near
    factor = math.log2(math.e) / math.sqrt(HD)
    near_spec = pl.BlockSpec((2, None, near, HD), lambda h, t: (0, h, 0, 0))
    part = rows // parts
    return pl.pallas_call(
        functools.partial(space_attend_kernel, factor, parts),
        out_shape=jax.ShapeDtypeStruct((parts, count, part, HD), jnp.bfloat16),
        grid_spec=pltpu.PrefetchScalarGridSpec(
            num_scalar_prefetch=1,
            grid=(count,),
            in_specs=[
                pl.BlockSpec((None, None, rows, HD), lambda h, t: (0, h, 0, 0)),
                pl.BlockSpec((2, None, rows, HD), lambda h, t: (0, h, 0, 0)),
                near_spec,
                near_spec,
                pl.BlockSpec((None, total // BLOCK, HD), lambda h, t: (h, 0, 0)),
                pl.BlockSpec(memory_space=pl.ANY),
            ],
            out_specs=pl.BlockSpec((parts, None, part, HD), lambda h, t: (0, h, 0, 0)),
            scratch_shapes=[
                pltpu.VMEM((total, 2 * HD), jnp.bfloat16),
                pltpu.VMEM((total, 2 * HD), jnp.bfloat16),
                pltpu.VMEM((rows, HD), jnp.bfloat16),
            ],
        ),
        compiler_params=pltpu.CompilerParams(vmem_limit_bytes=VMEM_LIMIT),
        cost_estimate=pl.CostEstimate(
            flops=8 * count * rows * total * HD,
            bytes_accessed=2 * HD * count * (4 * rows + 4 * near),
            transcendentals=count * rows * total,
        ),
        name="space_attend",
    )(side, q, kv, prev_kv, next_kv, bias, after)


def time_attend_kernel(factor, blocks, mask, x_ref, after_ref, out_ref, ka, va):
    frames, _, pos, _ = x_ref.shape
    rows = frames * pos
    span = pos * (BLOCK // STRIP)
    head = pl.program_id(0)
    ka[:, :HD] = x_ref[:, 1].reshape(rows, HD)
    va[:, :HD] = x_ref[:, 2].reshape(rows, HD)
    va[:, HD:] = jnp.ones((rows, HD), jnp.bfloat16)
    row = lax.broadcasted_iota(jnp.int32, (rows, HD), 0)
    lane = lax.broadcasted_iota(jnp.int32, (rows, HD), 1)
    strip = lax.rem(row, pos) // STRIP
    block = row // span
    lane_strip, lane_block = lane // blocks, lax.rem(lane, blocks)
    live = jnp.zeros((rows, HD), jnp.float32)
    for a in range(blocks):
        for b in range(blocks):
            m = mask[(head * blocks + a) * blocks + b].astype(jnp.float32)
            live = jnp.where((lane_block == a) & (block == b), m, live)
    live = jnp.where(strip == lane_strip, live, 0.0)
    ka[:, HD:] = ((live - 1.0) * BIG).astype(jnp.bfloat16)
    marks = jnp.where(strip * blocks + block == lane, 1.0, 0.0).astype(jnp.bfloat16)
    queries = jnp.concatenate([x_ref[:, 0].reshape(rows, HD), marks], axis=1)
    step = chunk_rows(rows, 256)
    per = step // pos
    parts, q = out_ref.shape[1], out_ref.shape[2]
    for m in range(rows // step):
        result = attend_rows(queries[m * step : (m + 1) * step], ka[...], va[...], factor)
        out_ref[m * per : (m + 1) * per] = result.reshape(per, parts, q, HD)


def time_attend(received, mask, after, deal):
    frames, _, count, pos, _ = received.shape
    rows = frames * pos
    factor = math.log2(math.e) / math.sqrt(HD)
    return pl.pallas_call(
        functools.partial(time_attend_kernel, factor, mask.shape[1]),
        out_shape=jax.ShapeDtypeStruct((frames, deal, count, pos // deal, HD), jnp.bfloat16),
        grid_spec=pltpu.PrefetchScalarGridSpec(
            num_scalar_prefetch=1,
            grid=(count,),
            in_specs=[
                pl.BlockSpec((frames, 3, None, pos, HD), lambda h, t: (0, 0, h, 0, 0)),
                pl.BlockSpec(memory_space=pl.ANY),
            ],
            out_specs=pl.BlockSpec((frames, deal, None, pos // deal, HD), lambda h, t: (0, 0, h, 0, 0)),
            scratch_shapes=[
                pltpu.VMEM((rows, 2 * HD), jnp.bfloat16),
                pltpu.VMEM((rows, 2 * HD), jnp.bfloat16),
            ],
        ),
        compiler_params=pltpu.CompilerParams(vmem_limit_bytes=VMEM_LIMIT),
        cost_estimate=pl.CostEstimate(
            flops=8 * count * rows * rows * HD,
            bytes_accessed=8 * HD * count * rows,
            transcendentals=count * rows * rows,
        ),
        name="time_attend",
    )(mask.reshape(-1), received, after)


def place_space_kernel(sources, table, *refs):
    h = pl.program_id(0)
    chosen = table[pl.num_programs(0) + h]
    out_ref = refs[-1]
    for n in range(sources):

        @pl.when(chosen == n)
        def _():
            out_ref[...] = refs[n][...]


def place_space(columns, chosen, sources, width):
    count = columns.shape[0]
    rows = sources[0][0].shape[1]

    def spec(n):
        return pl.BlockSpec((None, rows, HD), lambda h, t: (t[(2 + n) * count + h], 0, 0))

    return pl.pallas_call(
        functools.partial(place_space_kernel, len(sources)),
        out_shape=jax.ShapeDtypeStruct((rows, width), jnp.bfloat16),
        grid_spec=pltpu.PrefetchScalarGridSpec(
            num_scalar_prefetch=1,
            grid=(count,),
            in_specs=[spec(n) for n in range(len(sources))],
            out_specs=pl.BlockSpec((rows, HD), lambda h, t: (0, t[h])),
        ),
        cost_estimate=pl.CostEstimate(flops=0, bytes_accessed=4 * rows * count * HD, transcendentals=0),
        name="place_space",
    )(jnp.concatenate([columns, chosen] + [at for _, at in sources]), *[array for array, _ in sources])


def place_time_kernel(table, timed_ref, placed_ref, out_ref):
    out_ref[...] = timed_ref[...].reshape(out_ref.shape)


def place_time(columns, timed, block, index, placed):
    rows = placed.shape[0]
    return pl.pallas_call(
        place_time_kernel,
        out_shape=jax.ShapeDtypeStruct(placed.shape, placed.dtype),
        grid_spec=pltpu.PrefetchScalarGridSpec(
            num_scalar_prefetch=1,
            grid=(columns.shape[0],),
            in_specs=[pl.BlockSpec(block, index), pl.BlockSpec(memory_space=pl.ANY)],
            out_specs=pl.BlockSpec((rows, HD), lambda g, t: (0, t[g])),
        ),
        input_output_aliases={2: 0},
        cost_estimate=pl.CostEstimate(
            flops=0, bytes_accessed=4 * rows * columns.shape[0] * HD, transcendentals=0
        ),
        name="place_time",
    )(columns, timed, placed)


def block_picks(live):
    used = jnp.max(live, axis=1)
    width = used.shape[1]
    before = (jnp.arange(width)[:, None] < jnp.arange(width)[None, :]).astype(jnp.int32)
    rank = jnp.sum(used[:, :, None] * before[None], axis=1)
    return used[:, None, :] * (rank[:, None, :] == jnp.arange(NEAR_MAX)[None, :, None]).astype(jnp.int32)


def on_device(tokens, qkv_weight, query_gain, key_gain, labels, space_mask, time_mask):
    frame_count = lax.axis_size("frame")
    sides = lax.axis_size("head")
    own_frame = lax.axis_index("frame")
    own_side = lax.axis_index("head")
    row_count = tokens.shape[0]
    groups = labels.shape[0] // 3
    blocks = row_count // BLOCK
    space_count = 2 * groups
    gq, gk = query_gain.reshape(1, HD), key_gain.reshape(1, HD)

    picked = labels.reshape(groups, 3)
    time_slot = jnp.sum(picked * jnp.arange(3, dtype=jnp.int32)[None, :], axis=1)
    group_base = 3 * jnp.arange(groups, dtype=jnp.int32)
    time_heads = group_base + time_slot
    first_space = group_base + jnp.where(time_slot == 0, 1, 0)
    second_space = group_base + jnp.where(time_slot == 2, 1, 2)
    space_heads = jnp.stack([first_space, second_space], axis=1).reshape(space_count)

    live = jnp.take(space_mask, space_heads, axis=0)
    low, own, high = live[:, :, :blocks], live[:, :, blocks : 2 * blocks], live[:, :, 2 * blocks :]
    low_pick, high_pick = block_picks(low), block_picks(high)
    ids = jnp.arange(blocks, dtype=jnp.int32)
    picks = jnp.stack([jnp.sum(low_pick * ids, axis=-1), jnp.sum(high_pick * ids, axis=-1)], axis=1)
    low_ok = (own_frame > 0).astype(jnp.int32)
    high_ok = (own_frame < frame_count - 1).astype(jnp.int32)

    def near_live(pick, side, ok):
        return ok * jnp.sum(pick[:, :, None, :] * side[:, None, :, :], axis=-1)

    allowed = jnp.concatenate(
        [jnp.swapaxes(own, 1, 2), near_live(low_pick, low, low_ok), near_live(high_pick, high, high_ok)],
        axis=1,
    )
    bias = jnp.pad((allowed.astype(jnp.float32) - 1.0) * BIG, ((0, 0), (0, 0), (0, HD - blocks)))

    pos_count = row_count // frame_count
    deal = sides if pos_count % (sides * STRIP) == 0 else 1
    up = [(i, i + 1) for i in range(frame_count - 1)]
    down = [(i + 1, i) for i in range(frame_count - 1)]
    swap = [(0, 1), (1, 0)]
    kv, to_next, to_prev = project(tokens, qkv_weight, gq, gk, space_heads, (1, 2), gq, picks=picks)
    prev_kv = lax.ppermute(to_next, "frame", up)
    next_kv = lax.ppermute(to_prev, "frame", down)
    packed = project(tokens, qkv_weight, gq, gk, time_heads, (0, 1, 2), kv, strips=frame_count, deal=deal)
    received = lax.all_to_all(packed, "frame", split_axis=0, concat_axis=0, tiled=True)
    query_heads = space_heads
    if sides == 2:
        their_slot = lax.ppermute(time_slot, "head", swap)
        query_heads, their_slot = lax.optimization_barrier((space_heads, their_slot))
        slots = jnp.where(
            own_side == 0,
            jnp.concatenate([time_slot, their_slot]),
            jnp.concatenate([their_slot, time_slot]),
        )
    else:
        slots = lax.all_to_all(
            jnp.broadcast_to(time_slot[None], (sides, groups)), "head", 0, 0, tiled=True
        ).reshape(-1)
    space_q = project(tokens, qkv_weight, gq, gk, query_heads, (0,), packed)

    side = jnp.reshape(own_side if sides == 2 else jnp.int32(0), (1,)).astype(jnp.int32)
    space_out = space_attend(space_q, kv, prev_kv, next_kv, bias, sides, side, space_q)
    mask = jnp.take(time_mask, time_heads, axis=0)
    time_out = time_attend(received, mask, space_out, deal)

    part_rows = row_count // sides
    total_heads = sides * space_count
    head_ids = jnp.arange(total_heads, dtype=jnp.int32)
    if sides == 2:
        space_recv = lax.ppermute(space_out[1], "head", swap)

        def clamped(whose):
            return jnp.clip(head_ids - whose * space_count, 0, space_count - 1)

        sources = [(space_out[0], clamped(own_side)), (space_recv, clamped(1 - own_side))]
        chosen = (head_ids // space_count != own_side).astype(jnp.int32)
    else:
        space_all = lax.all_to_all(space_out, "head", 0, 0, tiled=True)
        sources = [(space_all.reshape(total_heads, part_rows, HD), head_ids)]
        chosen = jnp.zeros_like(head_ids)
    all_groups = jnp.arange(sides * groups, dtype=jnp.int32)
    firsts = 3 * all_groups + jnp.where(slots == 0, 1, 0)
    seconds = 3 * all_groups + jnp.where(slots == 2, 1, 2)
    space_columns = jnp.stack([firsts, seconds], axis=1).reshape(total_heads)
    placed = place_space(space_columns, chosen, sources, sides * groups * 3 * HD)

    if deal == sides:
        q = pos_count // sides
        timed = lax.all_to_all(
            time_out.reshape(frame_count * sides, groups, q, HD), ("frame", "head"), 0, 0, tiled=True
        )
        timed = timed.reshape(frame_count, sides, groups, q, HD)
        block = (frame_count, None, None, q, HD)

        def index(g, t):
            return (0, g // groups, lax.rem(g, groups), 0, 0)

    else:
        timed = time_out.reshape(frame_count, groups, pos_count, HD)
        timed = lax.all_to_all(timed, "frame", 0, 0, tiled=True)
        timed = lax.all_to_all(timed, "head", 0, 0, tiled=True)
        timed = timed.reshape(sides, frame_count // sides, groups, pos_count, HD)
        block = (None, frame_count // sides, None, pos_count, HD)

        def index(g, t):
            return (g // groups, 0, lax.rem(g, groups), 0, 0)

    return place_time(3 * all_groups + slots, timed, block, index, placed)


def solution(mesh):
    placed = (
        P("frame", None),
        P(None, None, "head"),
        P(),
        P(),
        P("head"),
        P("head", None, None),
        P("head", None, None),
    )

    return jax.shard_map(on_device, mesh=mesh, in_specs=placed, out_specs=P(("frame", "head"), None), check_vma=False)
```

```python
import functools
import math

import jax
import jax.numpy as jnp
from jax import lax
from jax.experimental import pallas as pl
from jax.experimental.pallas import tpu as pltpu
from jax.sharding import PartitionSpec as P


STRIP = 8
BLOCK = 64
NEAR_MAX = 8
HD = 128
epsilon = 1e-06
BIG = 1e30
VMEM_LIMIT = 56 * 1024 * 1024


def chunk_rows(rows, want):
    while rows % want:
        want //= 2
    return want


def normed_head(projected, gains):
    inverse_rms = lax.rsqrt(jnp.mean(projected * projected, axis=-1, keepdims=True) + epsilon)
    return (projected * inverse_rms * gains).astype(jnp.bfloat16)


def project_kernel(kinds, pair, near_count, strips, table, x_ref, gq_ref, gk_ref, after_ref, *refs):
    weights = refs[: len(kinds) * pair]
    outs = refs[len(kinds) * pair :]
    out_ref = outs[0]
    i = pl.program_id(0)
    count = pl.num_programs(0) * pair
    step = x_ref.shape[0] // strips if strips > 1 else chunk_rows(x_ref.shape[0], 512)
    gains = {0: gq_ref[...], 1: gk_ref[...]}

    def body(m, carry):
        rows = pl.ds(pl.multiple_of(m * step, step), step)
        x = x_ref[rows, :]
        for n, kind in enumerate(kinds):
            w = [w_ref[...] for w_ref in weights[n * pair : (n + 1) * pair]]
            w = w[0] if pair == 1 else jnp.concatenate(w, axis=1)
            product = jnp.dot(x, w, preferred_element_type=jnp.float32)
            for j in range(pair):
                part = product[:, j * HD : (j + 1) * HD]
                if kind in gains:
                    part = normed_head(part, gains[kind])
                else:
                    part = part.astype(jnp.bfloat16)
                if strips:
                    pos = out_ref.shape[3]
                    if strips == 1:
                        per = step // pos
                        out_ref[pl.ds(m * per, per), n, j] = part.reshape(per, pos, HD)
                    else:
                        q = pos // strips
                        at = pl.ds(pl.multiple_of(m * q, q), q)
                        out_ref[:, n, j, at, :] = part.reshape(out_ref.shape[0], q, HD)
                else:
                    out_ref[n, j, rows, :] = part
        return carry

    lax.fori_loop(0, x_ref.shape[0] // step, body, 0)
    for j in range(pair if near_count else 0):
        head = i * pair + j
        for s in range(near_count):
            for side, ref in ((0, outs[1]), (1, outs[2])):
                b = table[count + (head * 2 + side) * near_count + s]
                src = pl.ds(pl.multiple_of(b * BLOCK, BLOCK), BLOCK)
                for n in range(2):
                    ref[n, j, s * BLOCK : (s + 1) * BLOCK, :] = out_ref[n, j, src, :]


def project(tokens, weight, gq, gk, heads, kinds, after, strips=0, deal=1, picks=None):
    rows, d = tokens.shape
    count = heads.shape[0]
    pair = 2 if count % 2 == 0 else 1
    n = len(kinds)
    near_count = 0 if picks is None else NEAR_MAX
    table = heads if picks is None else jnp.concatenate([heads, picks.reshape(-1)])

    def w_spec(kind, j):
        return pl.BlockSpec((None, d, HD), lambda i, t: (kind, 0, t[pair * i + j]))

    gain = pl.BlockSpec((1, HD), lambda i, t: (0, 0))
    if strips:
        pos = rows // strips
        shapes = [jax.ShapeDtypeStruct((strips, n, count, pos, HD), jnp.bfloat16)]
        specs = [pl.BlockSpec((strips, n, pair, pos, HD), lambda i, t: (0, 0, i, 0, 0))]
    else:
        shapes = [jax.ShapeDtypeStruct((n, count, rows, HD), jnp.bfloat16)]
        specs = [pl.BlockSpec((n, pair, rows, HD), lambda i, t: (0, i, 0, 0))]
    if near_count:
        near = near_count * BLOCK
        shapes += [jax.ShapeDtypeStruct((2, count, near, HD), jnp.bfloat16)] * 2
        specs += [pl.BlockSpec((2, pair, near, HD), lambda i, t: (0, i, 0, 0))] * 2
    out = pl.pallas_call(
        functools.partial(project_kernel, kinds, pair, near_count, deal if strips else 0),
        out_shape=tuple(shapes),
        grid_spec=pltpu.PrefetchScalarGridSpec(
            num_scalar_prefetch=1,
            grid=(count // pair,),
            in_specs=[
                pl.BlockSpec((rows, d), lambda i, t: (0, 0), pipeline_mode=pl.Buffered(1)),
                gain,
                gain,
                pl.BlockSpec(memory_space=pl.ANY),
            ]
            + [w_spec(kind, j) for kind in kinds for j in range(pair)],
            out_specs=tuple(specs),
        ),
        compiler_params=pltpu.CompilerParams(vmem_limit_bytes=VMEM_LIMIT),
        cost_estimate=pl.CostEstimate(
            flops=2 * rows * d * n * count * HD,
            bytes_accessed=2 * (rows * d + n * d * count * HD + n * rows * count * HD),
            transcendentals=0,
        ),
    )(table, tokens, gq, gk, after, *([weight] * (n * pair)))
    return out if near_count else out[0]


def attend_rows(queries, keys, values, factor):
    scores = lax.dot_general(
        queries, keys, (((1,), (1,)), ((), ())), preferred_element_type=jnp.float32
    )
    weight = jnp.exp2(scores * factor).astype(jnp.bfloat16)
    both = jnp.dot(weight, values, preferred_element_type=jnp.float32)
    return (both[:, :HD] / both[:, HD:]).astype(jnp.bfloat16)


def space_attend_kernel(factor, parts, side, q_ref, kv_ref, prev_ref, next_ref, bias_ref, after_ref, out_ref, ka, va, marks):
    rows = q_ref.shape[0]
    near = prev_ref.shape[1]
    total = rows + 2 * near

    @pl.when(pl.program_id(0) == 0)
    def _():
        va[:, HD:] = jnp.ones((total, HD), jnp.bfloat16)
        row = lax.broadcasted_iota(jnp.int32, (rows, HD), 0) // BLOCK
        lane = lax.broadcasted_iota(jnp.int32, (rows, HD), 1)
        marks[...] = jnp.where(row == lane, 1.0, 0.0).astype(jnp.bfloat16)

    for slot, ref in ((0, ka), (1, va)):
        ref[:rows, :HD] = kv_ref[slot]
        ref[rows : rows + near, :HD] = prev_ref[slot]
        ref[rows + near :, :HD] = next_ref[slot]
    for b in range(total // BLOCK):
        ka[b * BLOCK : (b + 1) * BLOCK, HD:] = jnp.broadcast_to(
            bias_ref[b : b + 1, :], (BLOCK, HD)
        ).astype(jnp.bfloat16)
    part = rows // parts
    step = chunk_rows(part, 256)
    for m in range(rows // step):
        span = slice(m * step, (m + 1) * step)
        queries = jnp.concatenate([q_ref[span, :], marks[span, :]], axis=1)
        result = attend_rows(queries, ka[...], va[...], factor)
        which = lax.rem(m * step // part - side[0] + parts, parts)
        first = m * step % part
        out_ref[which, first : first + step, :] = result


def space_attend(q, kv, prev_kv, next_kv, bias, parts, side, after):
    count = q.shape[1]
    rows = q.shape[2]
    near = prev_kv.shape[2]
    total = rows + 2 * near
    factor = math.log2(math.e) / math.sqrt(HD)
    near_spec = pl.BlockSpec((2, None, near, HD), lambda h, t: (0, h, 0, 0))
    part = rows // parts
    return pl.pallas_call(
        functools.partial(space_attend_kernel, factor, parts),
        out_shape=jax.ShapeDtypeStruct((parts, count, part, HD), jnp.bfloat16),
        grid_spec=pltpu.PrefetchScalarGridSpec(
            num_scalar_prefetch=1,
            grid=(count,),
            in_specs=[
                pl.BlockSpec((None, None, rows, HD), lambda h, t: (0, h, 0, 0)),
                pl.BlockSpec((2, None, rows, HD), lambda h, t: (0, h, 0, 0)),
                near_spec,
                near_spec,
                pl.BlockSpec((None, total // BLOCK, HD), lambda h, t: (h, 0, 0)),
                pl.BlockSpec(memory_space=pl.ANY),
            ],
            out_specs=pl.BlockSpec((parts, None, part, HD), lambda h, t: (0, h, 0, 0)),
            scratch_shapes=[
                pltpu.VMEM((total, 2 * HD), jnp.bfloat16),
                pltpu.VMEM((total, 2 * HD), jnp.bfloat16),
                pltpu.VMEM((rows, HD), jnp.bfloat16),
            ],
        ),
        compiler_params=pltpu.CompilerParams(vmem_limit_bytes=VMEM_LIMIT),
        cost_estimate=pl.CostEstimate(
            flops=8 * count * rows * total * HD,
            bytes_accessed=2 * HD * count * (4 * rows + 4 * near),
            transcendentals=count * rows * total,
        ),
        name="space_attend",
    )(side, q, kv, prev_kv, next_kv, bias, after)


def time_attend_kernel(factor, blocks, mask, x_ref, after_ref, out_ref, ka, va):
    frames, _, pos, _ = x_ref.shape
    rows = frames * pos
    span = pos * (BLOCK // STRIP)
    head = pl.program_id(0)
    ka[:, :HD] = x_ref[:, 1].reshape(rows, HD)
    va[:, :HD] = x_ref[:, 2].reshape(rows, HD)
    va[:, HD:] = jnp.ones((rows, HD), jnp.bfloat16)
    row = lax.broadcasted_iota(jnp.int32, (rows, HD), 0)
    lane = lax.broadcasted_iota(jnp.int32, (rows, HD), 1)
    strip = lax.rem(row, pos) // STRIP
    block = row // span
    lane_strip, lane_block = lane // blocks, lax.rem(lane, blocks)
    live = jnp.zeros((rows, HD), jnp.float32)
    for a in range(blocks):
        for b in range(blocks):
            m = mask[(head * blocks + a) * blocks + b].astype(jnp.float32)
            live = jnp.where((lane_block == a) & (block == b), m, live)
    live = jnp.where(strip == lane_strip, live, 0.0)
    ka[:, HD:] = ((live - 1.0) * BIG).astype(jnp.bfloat16)
    marks = jnp.where(strip * blocks + block == lane, 1.0, 0.0).astype(jnp.bfloat16)
    queries = jnp.concatenate([x_ref[:, 0].reshape(rows, HD), marks], axis=1)
    step = chunk_rows(rows, 256)
    per = step // pos
    parts, q = out_ref.shape[1], out_ref.shape[2]
    for m in range(rows // step):
        result = attend_rows(queries[m * step : (m + 1) * step], ka[...], va[...], factor)
        out_ref[m * per : (m + 1) * per] = result.reshape(per, parts, q, HD)


def time_attend(received, mask, after, deal):
    frames, _, count, pos, _ = received.shape
    rows = frames * pos
    factor = math.log2(math.e) / math.sqrt(HD)
    return pl.pallas_call(
        functools.partial(time_attend_kernel, factor, mask.shape[1]),
        out_shape=jax.ShapeDtypeStruct((frames, deal, count, pos // deal, HD), jnp.bfloat16),
        grid_spec=pltpu.PrefetchScalarGridSpec(
            num_scalar_prefetch=1,
            grid=(count,),
            in_specs=[
                pl.BlockSpec((frames, 3, None, pos, HD), lambda h, t: (0, 0, h, 0, 0)),
                pl.BlockSpec(memory_space=pl.ANY),
            ],
            out_specs=pl.BlockSpec((frames, deal, None, pos // deal, HD), lambda h, t: (0, 0, h, 0, 0)),
            scratch_shapes=[
                pltpu.VMEM((rows, 2 * HD), jnp.bfloat16),
                pltpu.VMEM((rows, 2 * HD), jnp.bfloat16),
            ],
        ),
        compiler_params=pltpu.CompilerParams(vmem_limit_bytes=VMEM_LIMIT),
        cost_estimate=pl.CostEstimate(
            flops=8 * count * rows * rows * HD,
            bytes_accessed=8 * HD * count * rows,
            transcendentals=count * rows * rows,
        ),
        name="time_attend",
    )(mask.reshape(-1), received, after)


def place_space_kernel(sources, table, *refs):
    h = pl.program_id(0)
    chosen = table[pl.num_programs(0) + h]
    out_ref = refs[-1]
    for n in range(sources):

        @pl.when(chosen == n)
        def _():
            out_ref[...] = refs[n][...]


def place_space(columns, chosen, sources, width):
    count = columns.shape[0]
    rows = sources[0][0].shape[1]

    def spec(n):
        return pl.BlockSpec((None, rows, HD), lambda h, t: (t[(2 + n) * count + h], 0, 0))

    return pl.pallas_call(
        functools.partial(place_space_kernel, len(sources)),
        out_shape=jax.ShapeDtypeStruct((rows, width), jnp.bfloat16),
        grid_spec=pltpu.PrefetchScalarGridSpec(
            num_scalar_prefetch=1,
            grid=(count,),
            in_specs=[spec(n) for n in range(len(sources))],
            out_specs=pl.BlockSpec((rows, HD), lambda h, t: (0, t[h])),
        ),
        cost_estimate=pl.CostEstimate(flops=0, bytes_accessed=4 * rows * count * HD, transcendentals=0),
        name="place_space",
    )(jnp.concatenate([columns, chosen] + [at for _, at in sources]), *[array for array, _ in sources])


def place_time_kernel(pick, count, table, timed_ref, placed_ref, out_ref, held, sems):
    copies = []
    for g in range(count):
        held[g] = pick(timed_ref, g).reshape(held.shape[1:])
        column = pl.ds(pl.multiple_of(table[g] * HD, HD), HD)
        copies.append(pltpu.make_async_copy(held.at[g], out_ref.at[:, column], sems.at[g]))
        copies[-1].start()
    for copy in copies:
        copy.wait()


def place_time(columns, timed, pick, placed):
    rows = placed.shape[0]
    count = columns.shape[0]
    return pl.pallas_call(
        functools.partial(place_time_kernel, pick, count),
        out_shape=jax.ShapeDtypeStruct(placed.shape, placed.dtype),
        grid_spec=pltpu.PrefetchScalarGridSpec(
            num_scalar_prefetch=1,
            grid=(1,),
            in_specs=[
                pl.BlockSpec(memory_space=pltpu.VMEM),
                pl.BlockSpec(memory_space=pl.ANY),
            ],
            out_specs=pl.BlockSpec(memory_space=pl.ANY),
            scratch_shapes=[
                pltpu.VMEM((count, rows, HD), jnp.bfloat16),
                pltpu.SemaphoreType.DMA((count,)),
            ],
        ),
        input_output_aliases={2: 0},
        compiler_params=pltpu.CompilerParams(vmem_limit_bytes=16 * 1024 * 1024),
        cost_estimate=pl.CostEstimate(
            flops=0, bytes_accessed=4 * rows * count * HD, transcendentals=0
        ),
        name="place_time",
    )(columns, timed, placed)


def block_picks(live):
    used = jnp.max(live, axis=1)
    width = used.shape[1]
    before = (jnp.arange(width)[:, None] < jnp.arange(width)[None, :]).astype(jnp.int32)
    rank = jnp.sum(used[:, :, None] * before[None], axis=1)
    return used[:, None, :] * (rank[:, None, :] == jnp.arange(NEAR_MAX)[None, :, None]).astype(jnp.int32)


def on_device(tokens, qkv_weight, query_gain, key_gain, labels, space_mask, time_mask):
    frame_count = lax.axis_size("frame")
    sides = lax.axis_size("head")
    own_frame = lax.axis_index("frame")
    own_side = lax.axis_index("head")
    row_count = tokens.shape[0]
    groups = labels.shape[0] // 3
    blocks = row_count // BLOCK
    space_count = 2 * groups
    gq, gk = query_gain.reshape(1, HD), key_gain.reshape(1, HD)

    picked = labels.reshape(groups, 3)
    time_slot = jnp.sum(picked * jnp.arange(3, dtype=jnp.int32)[None, :], axis=1)
    group_base = 3 * jnp.arange(groups, dtype=jnp.int32)
    time_heads = group_base + time_slot
    first_space = group_base + jnp.where(time_slot == 0, 1, 0)
    second_space = group_base + jnp.where(time_slot == 2, 1, 2)
    space_heads = jnp.stack([first_space, second_space], axis=1).reshape(space_count)

    live = jnp.take(space_mask, space_heads, axis=0)
    low, own, high = live[:, :, :blocks], live[:, :, blocks : 2 * blocks], live[:, :, 2 * blocks :]
    low_pick, high_pick = block_picks(low), block_picks(high)
    ids = jnp.arange(blocks, dtype=jnp.int32)
    picks = jnp.stack([jnp.sum(low_pick * ids, axis=-1), jnp.sum(high_pick * ids, axis=-1)], axis=1)
    low_ok = (own_frame > 0).astype(jnp.int32)
    high_ok = (own_frame < frame_count - 1).astype(jnp.int32)

    def near_live(pick, side, ok):
        return ok * jnp.sum(pick[:, :, None, :] * side[:, None, :, :], axis=-1)

    allowed = jnp.concatenate(
        [jnp.swapaxes(own, 1, 2), near_live(low_pick, low, low_ok), near_live(high_pick, high, high_ok)],
        axis=1,
    )
    bias = jnp.pad((allowed.astype(jnp.float32) - 1.0) * BIG, ((0, 0), (0, 0), (0, HD - blocks)))

    pos_count = row_count // frame_count
    deal = sides if pos_count % (sides * STRIP) == 0 else 1
    up = [(i, i + 1) for i in range(frame_count - 1)]
    down = [(i + 1, i) for i in range(frame_count - 1)]
    swap = [(0, 1), (1, 0)]
    kv, to_next, to_prev = project(tokens, qkv_weight, gq, gk, space_heads, (1, 2), gq, picks=picks)
    prev_kv = lax.ppermute(to_next, "frame", up)
    next_kv = lax.ppermute(to_prev, "frame", down)
    packed = project(tokens, qkv_weight, gq, gk, time_heads, (0, 1, 2), kv, strips=frame_count, deal=deal)
    received = lax.all_to_all(packed, "frame", split_axis=0, concat_axis=0, tiled=True)
    query_heads = space_heads
    if sides == 2:
        their_slot = lax.ppermute(time_slot, "head", swap)
        query_heads, their_slot = lax.optimization_barrier((space_heads, their_slot))
        slots = jnp.where(
            own_side == 0,
            jnp.concatenate([time_slot, their_slot]),
            jnp.concatenate([their_slot, time_slot]),
        )
    else:
        slots = lax.all_to_all(
            jnp.broadcast_to(time_slot[None], (sides, groups)), "head", 0, 0, tiled=True
        ).reshape(-1)
    space_q = project(tokens, qkv_weight, gq, gk, query_heads, (0,), packed)

    side = jnp.reshape(own_side if sides == 2 else jnp.int32(0), (1,)).astype(jnp.int32)
    space_out = space_attend(space_q, kv, prev_kv, next_kv, bias, sides, side, space_q)
    mask = jnp.take(time_mask, time_heads, axis=0)
    time_out = time_attend(received, mask, space_out, deal)

    part_rows = row_count // sides
    total_heads = sides * space_count
    head_ids = jnp.arange(total_heads, dtype=jnp.int32)
    if sides == 2:
        space_recv = lax.ppermute(space_out[1], "head", swap)

        def clamped(whose):
            return jnp.clip(head_ids - whose * space_count, 0, space_count - 1)

        sources = [(space_out[0], clamped(own_side)), (space_recv, clamped(1 - own_side))]
        chosen = (head_ids // space_count != own_side).astype(jnp.int32)
    else:
        space_all = lax.all_to_all(space_out, "head", 0, 0, tiled=True)
        sources = [(space_all.reshape(total_heads, part_rows, HD), head_ids)]
        chosen = jnp.zeros_like(head_ids)
    all_groups = jnp.arange(sides * groups, dtype=jnp.int32)
    firsts = 3 * all_groups + jnp.where(slots == 0, 1, 0)
    seconds = 3 * all_groups + jnp.where(slots == 2, 1, 2)
    space_columns = jnp.stack([firsts, seconds], axis=1).reshape(total_heads)
    placed = place_space(space_columns, chosen, sources, sides * groups * 3 * HD)

    if deal == sides:
        q = pos_count // sides
        timed = lax.all_to_all(
            time_out.reshape(frame_count * sides, groups, q, HD), ("frame", "head"), 0, 0, tiled=True
        )
        timed = timed.reshape(frame_count, sides, groups, q, HD)

        def pick(ref, g):
            return ref[:, g // groups, g % groups]

    else:
        timed = time_out.reshape(frame_count, groups, pos_count, HD)
        timed = lax.all_to_all(timed, "frame", 0, 0, tiled=True)
        timed = lax.all_to_all(timed, "head", 0, 0, tiled=True)
        timed = timed.reshape(sides, frame_count // sides, groups, pos_count, HD)

        def pick(ref, g):
            return ref[g // groups, :, g % groups]

    return place_time(3 * all_groups + slots, timed, pick, placed)


def solution(mesh):
    placed = (
        P("frame", None),
        P(None, None, "head"),
        P(),
        P(),
        P("head"),
        P("head", None, None),
        P("head", None, None),
    )

    return jax.shard_map(on_device, mesh=mesh, in_specs=placed, out_specs=P(("frame", "head"), None), check_vma=False)
```
